32 devices in a mesh: gx: 4 (over y, x), gy: 4 (over z), gz: 2 (over core).
Axes of the slice: x: 2, y: 2, z: 4, core: 2. Of those that a mesh axis runs over, the one named last changes fastest.
Arguments:
- provisional: float32 [9, 128, 64, 256], P(None, 'gx', 'gy', 'gz'), may hold values from -6 to 6
- cut_flag: int32 [128, 64, 256], P('gx', 'gy', 'gz'), may hold values from 0 to 1, as said below
- cut_code: int32 [128, 64, 256], P('gx', 'gy', 'gz'), may hold values from 0 to 134217727
- volume_level: int32 [128, 64, 256], P('gx', 'gy', 'gz'), may hold values from 1 to 256
- area_level: int32 [128, 64, 256], P('gx', 'gy', 'gz'), may hold values from 64 to 256
Outputs:
- redistributed: float32 [9, 128, 64, 256], P(None, 'gx', 'gy', 'gz')
- species_change: float32 [9], replicated
The draws below stay inside these ranges and needn't reach their ends.
Inputs may be any that keep to these rules, and one draw needn't show every extreme that they name: cut_flag marks the cells crossed by one closed embedded surface.
All inputs are finite; a program needn't handle non-finite values.
Results may differ from the reference program's by a relative error of at most 0.00002.
Values sent between devices are 32-bit elements; how exact they have to be, the bound alone decides.
A program may use at most 128 MiB of HBM per device.

```python
import math
import jax
import jax.numpy as jnp
from jax import lax

NSPEC = 9
NX = 128
NY = 64
NZ = 256


def draw_cut_flag(key, part):
    keys = jax.random.split(jax.random.fold_in(key, 7), 2)
    centre = jax.random.randint(keys[0], (3,), -128, 129)
    radius = jax.random.randint(keys[1], (), 200, 360)
    coord_x = (2 * jnp.arange(NX, dtype=jnp.int32) + 1) * 512 // NX - 512 - centre[0]
    coord_y = (2 * jnp.arange(NY, dtype=jnp.int32) + 1) * 512 // NY - 512 - centre[1]
    coord_z = (2 * jnp.arange(NZ, dtype=jnp.int32) + 1) * 512 // NZ - 512 - centre[2]
    distance = coord_x[:, None, None] * coord_x[:, None, None] + coord_y[None, :, None] * coord_y[None, :, None] + coord_z[None, None, :] * coord_z[None, None, :]
    spacing = max(max(1024 // NX, 1024 // NY), max(1024 // NZ, 1))
    band_width = 2 * radius * spacing
    shell = jnp.abs(distance - radius * radius) <= band_width
    return shell.astype(jnp.int32)


def set_ends(drawn, stream_key, least, high):
    index_at = [jax.random.randint(jax.random.fold_in(stream_key, axis), (), 0, length) for axis, length in enumerate(drawn.shape)]
    main_axis = drawn.shape.index(max(drawn.shape))
    beside = index_at[:main_axis] + [(index_at[main_axis] + 1) % drawn.shape[main_axis]] + index_at[main_axis + 1:]
    return drawn.at[tuple(index_at)].set(least).at[tuple(beside)].set(high)


def levels(key, shape, pieces, least, high):
    level, own = 1.0, jax.random.fold_in(key, 6)
    for dim, parts in pieces:
        steps = jnp.exp(jax.random.uniform(jax.random.fold_in(own, dim), (parts,), jnp.float32, least / len(pieces), high / len(pieces)))
        level = level * jnp.repeat(steps, shape[dim] // parts).reshape([-1 if axis == dim else 1 for axis in range(len(shape))])
    return level


def gaussian(key, dims, deviation, reach, pieces=(), kind=jnp.bfloat16):
    array = deviation * jax.random.normal(key, dims, jnp.float32)
    if pieces:
        array = array * levels(key, dims, pieces, -0.22, 0.18)
    return jnp.clip(array, -reach, reach).astype(kind)


def setup_inputs(seed: int = 0) -> dict:
    arg_keys = jax.random.split(jax.random.key(seed), 6)
    return {
        "provisional": gaussian(arg_keys[0], (NSPEC, NX, NY, NZ), 1.0, 6.0, ((1, 4), (2, 4), (3, 2)), jnp.float32),
        "cut_flag": draw_cut_flag(jax.random.fold_in(arg_keys[5], 71), 0),
        "cut_code": set_ends(jax.random.randint(arg_keys[2], (NX, NY, NZ), 0, 134217728), jax.random.fold_in(arg_keys[2], 1), 0, 134217727).astype(jnp.int32),
        "volume_level": set_ends(jax.random.randint(arg_keys[3], (NX, NY, NZ), 1, 257), jax.random.fold_in(arg_keys[3], 1), 1, 256).astype(jnp.int32),
        "area_level": set_ends(jax.random.randint(arg_keys[4], (NX, NY, NZ), 64, 257), jax.random.fold_in(arg_keys[4], 1), 64, 256).astype(jnp.int32),
    }


CENTER = 8192
OFFSETS = [(a, b, c) for a in (-1, 0, 1) for b in (-1, 0, 1) for c in (-1, 0, 1)]

def window(values, a, b, c, margin, border):
    extent_x = values.shape[-3] - 2 * border + 2 * margin
    extent_y = values.shape[-2] - 2 * border + 2 * margin
    extent_z = values.shape[-1] - 2 * border + 2 * margin
    start_x = border - margin + a
    start_y = border - margin + b
    start_z = border - margin + c
    return values[..., start_x:start_x + extent_x, start_y:start_y + extent_y, start_z:start_z + extent_z]

def member(codes, position):
    return (codes >> position & 1).astype(jnp.float32)

def reference(provisional, cut_flag, cut_code, volume_level, area_level):
    is_cut = cut_flag == 1
    codes = jnp.where(is_cut, cut_code | CENTER, CENTER)
    volume_frac = jnp.where(is_cut, volume_level, 256).astype(jnp.float32) / 256.0
    face_frac = jnp.where(is_cut, area_level, 256).astype(jnp.float32) / 256.0
    code_pad = jnp.pad(codes, 1) | CENTER
    counted = jnp.zeros(codes.shape, jnp.float32)
    for position, (a, b, c) in enumerate(OFFSETS):
        counted = counted + member(window(code_pad, -a, -b, -c, 0, 1), position)
    weights = volume_frac / counted
    portions = volume_frac * face_frac / counted
    portion_pad = jnp.pad(portions, 1)
    gathered = jnp.zeros(codes.shape, jnp.float32)
    for position, (a, b, c) in enumerate(OFFSETS):
        gathered = gathered + member(codes, position) * window(portion_pad, a, b, c, 0, 1)
    scaling = face_frac / counted

    def spread_species(values):
        carried = jnp.pad(weights * values, 1)
        amounts = jnp.zeros(codes.shape, jnp.float32)
        for position, (a, b, c) in enumerate(OFFSETS):
            amounts = amounts + member(codes, position) * window(carried, a, b, c, 0, 1)
        quotas = jnp.pad(amounts / gathered, 1)
        summed = jnp.zeros(codes.shape, jnp.float32)
        for position, (a, b, c) in enumerate(OFFSETS):
            summed = summed + member(window(code_pad, -a, -b, -c, 0, 1), position) * window(quotas, -a, -b, -c, 0, 1)
        return scaling * summed
    redistributed = lax.map(spread_species, provisional)
    species_change = lax.optimization_barrier(jnp.sum(volume_frac[None] * redistributed, axis=(1, 2, 3))) / math.sqrt(NX * NY * NZ)
    return (redistributed, species_change)
```

```python
import functools
import math

import jax
import jax.numpy as jnp
from jax import lax
from jax.experimental import pallas as pl
from jax.experimental.pallas import tpu as pltpu
from jax.sharding import PartitionSpec as P

CENTER = 8192
OFFSETS = [(a, b, c) for a in (-1, 0, 1) for b in (-1, 0, 1) for c in (-1, 0, 1)]
AXES = ("gx", "gy", "gz")
MESH = pl.DeviceIdType.MESH
LANES = 128
TILE = 8


def kernel(
    nx, ny, scale,
    prov, flag, code, vol, area,
    out, change,
    codes, codes_l, codes_r, carried, quotas, left, right, scaling,
    zs_i, zl_i, zr_i, zs_f, zl_f, zr_f, ys_i, yr_i, ys_f, yr_f, sums, peers,
    send, recv, peer_send, peer_recv,
):
    nspec = prov.shape[0]
    pitch = ny + TILE
    planes = nx + 2
    rows = TILE + planes * pitch
    tiles = ny // TILE
    here = {axis: lax.axis_index(axis) for axis in AXES}
    size = {axis: lax.axis_size(axis) for axis in AXES}
    lane = lax.broadcasted_iota(jnp.int32, (TILE, LANES), 1)

    barrier = pltpu.get_barrier_semaphore()
    for axis in AXES:
        for k in range(1, size[axis]):
            pl.semaphore_signal(
                barrier, inc=1, device_id={axis: lax.rem(here[axis] + k, size[axis])}, device_id_type=MESH
            )
    pl.semaphore_wait(barrier, sum(size[axis] - 1 for axis in AXES))

    def first(x):
        return TILE + x * pitch

    def own_tile(t):
        row = TILE + (t // tiles + 1) * pitch + lax.rem(t, tiles) * TILE
        return pl.multiple_of(row, TILE), pl.multiple_of(t * TILE, TILE)

    def links(axis, exchange, pairs):
        number = 2 * AXES.index(axis)
        n = size[axis]
        copies = []
        for way, (source, landing) in enumerate(pairs):
            step = 1 if way == 0 else n - 1
            copies.append(
                pltpu.make_async_remote_copy(
                    src_ref=source, dst_ref=landing,
                    send_sem=send.at[exchange, number + way], recv_sem=recv.at[exchange, number + way],
                    device_id={axis: lax.rem(here[axis] + step, n)}, device_id_type=MESH,
                )
            )
        return copies

    def has(axis):
        return here[axis] > 0, here[axis] < size[axis] - 1

    def start(axis, copies):
        below, above = has(axis)
        pl.when(above)(copies[0].start)
        pl.when(below)(copies[1].start)

    def finish(axis, copies):
        below, above = has(axis)
        pl.when(above)(copies[0].wait_send)
        pl.when(below)(copies[0].wait_recv)
        pl.when(below)(copies[1].wait_send)
        pl.when(above)(copies[1].wait_recv)

    def pack(packed, value, field):
        if packed is None:
            packed = jnp.zeros_like(value)
        keep = (lane == 2 * field) | (lane == (2 * field + LANES - 1) % LANES)
        rolled = value if field == 0 else pltpu.roll(value, 2 * field, 1)
        return jnp.where(keep, rolled, packed)

    def exchange(number, buf, zs, zl, zr, ys, yr, fields, between=None):
        zero = jnp.zeros((TILE, LANES), buf.dtype)
        z_copies = links("gz", number, ((zs, zl), (zs, zr)))
        start("gz", z_copies)
        finish("gz", z_copies)
        below, above = has("gz")
        odd = (lane & 1) == 1

        def place(t, carry):
            row, at = own_tile(t)
            low = jnp.where(below, zl[pl.ds(at, TILE), :], zero)
            high = jnp.where(above, zr[pl.ds(at, TILE), :], zero)
            buf[fields, pl.ds(row, TILE), :] = jnp.where(odd, low, high)
            return carry

        lax.fori_loop(0, nx * tiles, place, 0)
        x_copies = links(
            "gx", number,
            (
                (buf.at[:, pl.ds(first(nx), ny), :], buf.at[:, pl.ds(first(0), ny), :]),
                (buf.at[:, pl.ds(first(1), ny), :], buf.at[:, pl.ds(first(nx + 1), ny), :]),
            ),
        )
        start("gx", x_copies)
        if between is not None:
            between("gx")
        below, above = has("gx")

        def blank(x):
            for field in range(fields + 1):
                buf[field, pl.ds(first(x), ny), :] = jnp.zeros((ny, LANES), buf.dtype)

        pl.when(jnp.logical_not(below))(functools.partial(blank, 0))
        pl.when(jnp.logical_not(above))(functools.partial(blank, nx + 1))
        finish("gx", x_copies)

        chunks = [(x, min(TILE, planes - x)) for x in range(0, planes, TILE)]

        def gather(field, carry):
            for x, count in chunks:
                ys[0, field, pl.ds(x, count), :] = buf[field, pl.ds(first(x) + ny - 1, count, stride=pitch), :]
                ys[1, field, pl.ds(x, count), :] = buf[field, pl.ds(first(x), count, stride=pitch), :]
            return carry

        lax.fori_loop(0, fields + 1, gather, 0)
        y_copies = links("gy", number, ((ys.at[0], yr.at[0]), (ys.at[1], yr.at[1])))
        start("gy", y_copies)
        if between is not None:
            between("gy")
        finish("gy", y_copies)
        below, above = has("gy")

        def spread(field, carry):
            for x, count in chunks:
                blank_rows = jnp.zeros((count, LANES), buf.dtype)
                low = jnp.where(below, yr[0, field, pl.ds(x, count), :], blank_rows)
                high = jnp.where(above, yr[1, field, pl.ds(x, count), :], blank_rows)
                buf[field, pl.ds(first(x) - 1, count, stride=pitch), :] = low
                buf[field, pl.ds(first(x) + ny, count, stride=pitch), :] = high
            return carry

        lax.fori_loop(0, fields + 1, spread, 0)

    def shift(buf, to_left, to_right, fields):
        def body(t, carry):
            at = pl.ds(pl.multiple_of(t * TILE, TILE), TILE)
            ends = buf[fields, at, :]
            for field in range(fields):
                end = ends if field == 0 else pltpu.roll(ends, LANES - 2 * field, 1)
                value = buf[field, at, :]
                to_left[field, at, :] = pltpu.roll(jnp.where(lane == LANES - 1, end, value), 1, 1)
                to_right[field, at, :] = pltpu.roll(jnp.where(lane == 0, end, value), LANES - 1, 1)
            return carry

        lax.fori_loop(0, rows // TILE, body, 0)

    def fill(t, carry):
        row, at = own_tile(t)
        own = pl.ds(at, TILE)
        value = jnp.where(flag[own, :] == 1, code[own, :] | CENTER, CENTER)
        codes[0, pl.ds(row, TILE), :] = value
        zs_i[own, :] = pack(None, value, 0)
        return carry

    lax.fori_loop(0, nx * tiles, fill, 0)
    exchange(0, codes, zs_i, zl_i, zr_i, ys_i, yr_i, 1)
    shift(codes, codes_l, codes_r, 1)
    code_at = {-1: codes_l, 0: codes, 1: codes_r}

    sums[...] = jnp.zeros(sums.shape, jnp.float32)

    def weigh(t, carry):
        row, at = own_tile(t)
        own = pl.ds(at, TILE)
        counted = jnp.zeros((TILE, LANES), jnp.int32)
        for position, (a, b, c) in enumerate(OFFSETS):
            near = code_at[-c][0, pl.ds(row - a * pitch - b, TILE), :]
            counted = counted + (lax.shift_right_logical(near, position) & 1)
        is_cut = flag[own, :] == 1
        volume = jnp.where(is_cut, vol[own, :], 256).astype(jnp.float32) * (1.0 / 256.0)
        face = jnp.where(is_cut, area[own, :], 256).astype(jnp.float32) * (1.0 / 256.0)
        share = 1.0 / counted.astype(jnp.float32)
        scaling[own, :] = face * share
        weight = volume * share
        packed = None
        for s in range(nspec):
            p = prov[s, own, :]
            sums[s] = sums[s] + volume * p
            value = weight * p
            carried[s, pl.ds(row, TILE), :] = value
            packed = pack(packed, value, s)
        value = weight * face
        carried[nspec, pl.ds(row, TILE), :] = value
        zs_f[0, own, :] = pack(packed, value, nspec)
        return carry

    lax.fori_loop(0, nx * tiles, weigh, 0)

    def peer_copies(axis):
        n = size[axis]
        number = AXES.index(axis)
        return [
            pltpu.make_async_remote_copy(
                src_ref=peers.at[number, here[axis]], dst_ref=peers.at[number, here[axis]],
                send_sem=peer_send.at[number, k], recv_sem=peer_recv.at[number, k],
                device_id={axis: lax.rem(here[axis] + k, n)}, device_id_type=MESH,
            )
            for k in range(1, n)
        ]

    def total(axis):
        number = AXES.index(axis)
        value = peers[number, 0]
        for k in range(1, size[axis]):
            value = value + peers[number, k]
        return value

    def reduce_start(axis, value):
        peers[AXES.index(axis), here[axis]] = value
        for copy in peer_copies(axis):
            copy.start()

    def reduce_finish(axis):
        for copy in peer_copies(axis):
            copy.wait()
        return total(axis)

    local = jnp.concatenate(
        [jnp.sum(sums[s], axis=0, keepdims=True) for s in range(nspec)]
        + [jnp.zeros((peers.shape[2] - nspec, LANES), jnp.float32)],
        axis=0,
    )
    reduce_start("gx", local)

    def between(axis):
        if axis == "gx":
            reduce_start("gy", reduce_finish("gx"))
        else:
            reduce_start("gz", reduce_finish("gy"))

    exchange(1, carried, zs_f.at[0], zl_f.at[0], zr_f.at[0], ys_f.at[0], yr_f.at[0], nspec + 1, between)
    summed = reduce_finish("gz")
    change[...] = jnp.broadcast_to(jnp.sum(summed, axis=1, keepdims=True) * scale, change.shape)
    shift(carried, left, right, nspec + 1)
    carried_at = {-1: left, 0: carried, 1: right}

    def quota(t, carry):
        row, at = own_tile(t)
        mine = codes[0, pl.ds(row, TILE), :]
        zero = jnp.zeros((TILE, LANES), jnp.float32)
        totals = [zero] * (nspec + 1)
        for position, (a, b, c) in enumerate(OFFSETS):
            present = (mine & (1 << position)) != 0
            near = pl.ds(row + a * pitch + b, TILE)
            for s in range(nspec + 1):
                totals[s] = totals[s] + jnp.where(present, carried_at[c][s, near, :], zero)
        inverse = 1.0 / totals[nspec]
        packed = None
        for s in range(nspec):
            value = totals[s] * inverse
            quotas[s, pl.ds(row, TILE), :] = value
            packed = pack(packed, value, s)
        zs_f[1, pl.ds(at, TILE), :] = packed
        return carry

    lax.fori_loop(0, nx * tiles, quota, 0)
    exchange(
        2, quotas, zs_f.at[1], zl_f.at[1], zr_f.at[1],
        ys_f.at[1, :, pl.ds(0, nspec + 1)], yr_f.at[1, :, pl.ds(0, nspec + 1)], nspec,
    )
    shift(quotas, left, right, nspec)
    quotas_at = {-1: left, 0: quotas, 1: right}

    def scatter(t, carry):
        row, at = own_tile(t)
        own = pl.ds(at, TILE)
        zero = jnp.zeros((TILE, LANES), jnp.float32)
        totals = [zero] * nspec
        for position, (a, b, c) in enumerate(OFFSETS):
            near = pl.ds(row - a * pitch - b, TILE)
            present = (code_at[-c][0, near, :] & (1 << position)) != 0
            for s in range(nspec):
                totals[s] = totals[s] + jnp.where(present, quotas_at[-c][s, near, :], zero)
        factor = scaling[own, :]
        for s in range(nspec):
            out[s, own, :] = factor * totals[s]
        return carry

    lax.fori_loop(0, nx * tiles, scatter, 0)


def per_device(provisional, cut_flag, cut_code, volume_level, area_level):
    nspec, nx, ny, nz = provisional.shape
    assert nz == LANES and ny % TILE == 0
    own = nx * ny
    planes = nx + 2
    rows = TILE + planes * (ny + TILE)
    slab = -(-planes // TILE) * TILE
    most = max(lax.axis_size(axis) for axis in AXES)
    cells = own * nz * math.prod(lax.axis_size(axis) for axis in AXES)
    high = -(-nspec // TILE) * TILE
    f32, i32 = jnp.float32, jnp.int32
    vmem = pl.BlockSpec(memory_space=pltpu.VMEM)
    shapes = [
        ((2, rows, nz), i32), ((1, rows, nz), i32), ((1, rows, nz), i32),
        ((nspec + 2, rows, nz), f32), ((nspec + 1, rows, nz), f32),
        ((nspec + 1, rows, nz), f32), ((nspec + 1, rows, nz), f32),
        ((own, nz), f32),
        ((own, nz), i32), ((own, nz), i32), ((own, nz), i32),
        ((2, own, nz), f32), ((2, own, nz), f32), ((2, own, nz), f32),
        ((2, 2, slab, nz), i32), ((2, 2, slab, nz), i32),
        ((2, 2, nspec + 2, slab, nz), f32), ((2, 2, nspec + 2, slab, nz), f32),
        ((nspec, TILE, nz), f32), ((3, most, high, nz), f32),
    ]
    out, change = pl.pallas_call(
        functools.partial(kernel, nx, ny, 1.0 / math.sqrt(cells)),
        out_shape=(
            jax.ShapeDtypeStruct((nspec, own, nz), f32),
            jax.ShapeDtypeStruct((high, nz), f32),
        ),
        in_specs=[vmem] * 5,
        out_specs=(vmem, vmem),
        scratch_shapes=[pltpu.VMEM(shape, kind) for shape, kind in shapes]
        + [
            pltpu.SemaphoreType.DMA((3, 6)), pltpu.SemaphoreType.DMA((3, 6)),
            pltpu.SemaphoreType.DMA((3, most)), pltpu.SemaphoreType.DMA((3, most)),
        ],
        compiler_params=pltpu.CompilerParams(
            collective_id=0, has_side_effects=True, vmem_limit_bytes=60 * 1024 * 1024
        ),
    )(
        provisional.reshape(nspec, own, nz),
        cut_flag.reshape(own, nz),
        cut_code.reshape(own, nz),
        volume_level.reshape(own, nz),
        area_level.reshape(own, nz),
    )
    return out.reshape(provisional.shape), change[:nspec, 0]


def solution(mesh):
    spec = P("gx", "gy", "gz")
    wide = P(None, "gx", "gy", "gz")
    return jax.shard_map(
        per_device, mesh=mesh, in_specs=(wide, spec, spec, spec, spec), out_specs=(wide, P()), check_vma=False
    )
```

```python
import functools
import math

import jax
import jax.numpy as jnp
from jax import lax
from jax.experimental import pallas as pl
from jax.experimental.pallas import tpu as pltpu
from jax.sharding import PartitionSpec as P

CENTER = 8192
OFFSETS = [(a, b, c) for a in (-1, 0, 1) for b in (-1, 0, 1) for c in (-1, 0, 1)]
AXES = ("gx", "gy", "gz")
MESH = pl.DeviceIdType.MESH
LANES = 128
TILE = 8
GROUP = 4


def kernel(
    nx, ny, scale,
    prov, flag, code, vol, area,
    out, change,
    codes, codes_l, codes_r, carried_a, carried_b, quotas_a, quotas_b, left_a, right_a, left_b, right_b,
    scaling, weights, inverse,
    zs_i, zl_i, zr_i, zs_f, zl_f, zr_f, ys_i, yr_i, ys_f, yr_f, sums, peers,
    send, recv, peer_send, peer_recv,
):
    nspec = prov.shape[0]
    pitch = ny + TILE
    planes = nx + 2
    rows = codes.shape[1]
    tiles = ny // TILE
    here = {axis: lax.axis_index(axis) for axis in AXES}
    size = {axis: lax.axis_size(axis) for axis in AXES}
    lane = lax.broadcasted_iota(jnp.int32, (TILE, LANES), 1)

    barrier = pltpu.get_barrier_semaphore()
    for axis in AXES:
        for k in range(1, size[axis]):
            pl.semaphore_signal(
                barrier, inc=1, device_id={axis: lax.rem(here[axis] + k, size[axis])}, device_id_type=MESH
            )
    pl.semaphore_wait(barrier, sum(size[axis] - 1 for axis in AXES))

    def first(x):
        return TILE + x * pitch

    def own_tile(t):
        row = TILE + (t // tiles + 1) * pitch + lax.rem(t, tiles) * TILE
        return pl.multiple_of(row, TILE), pl.multiple_of(t * TILE, TILE)

    def links(axis, exchange, pairs):
        number = 2 * AXES.index(axis)
        n = size[axis]
        copies = []
        for way, (source, landing) in enumerate(pairs):
            step = 1 if way == 0 else n - 1
            copies.append(
                pltpu.make_async_remote_copy(
                    src_ref=source, dst_ref=landing,
                    send_sem=send.at[exchange, number + way], recv_sem=recv.at[exchange, number + way],
                    device_id={axis: lax.rem(here[axis] + step, n)}, device_id_type=MESH,
                )
            )
        return copies

    def has(axis):
        return here[axis] > 0, here[axis] < size[axis] - 1

    def start(axis, copies):
        below, above = has(axis)
        pl.when(above)(copies[0].start)
        pl.when(below)(copies[1].start)

    def finish(axis, copies):
        below, above = has(axis)
        pl.when(above)(copies[0].wait_send)
        pl.when(below)(copies[0].wait_recv)
        pl.when(below)(copies[1].wait_send)
        pl.when(above)(copies[1].wait_recv)

    def pack(packed, value, field):
        if packed is None:
            packed = jnp.zeros_like(value)
        keep = (lane == 2 * field) | (lane == (2 * field + LANES - 1) % LANES)
        rolled = value if field == 0 else pltpu.roll(value, 2 * field, 1)
        return jnp.where(keep, rolled, packed)

    def exchange(number, buf, zs, zl, zr, ys, yr, fields):
        zero = jnp.zeros((TILE, LANES), buf.dtype)
        z_copies = links("gz", number, ((zs, zl), (zs, zr)))
        start("gz", z_copies)
        yield
        finish("gz", z_copies)
        below, above = has("gz")
        odd = (lane & 1) == 1

        def place(t, carry):
            row, at = own_tile(t)
            low = jnp.where(below, zl[pl.ds(at, TILE), :], zero)
            high = jnp.where(above, zr[pl.ds(at, TILE), :], zero)
            buf[fields, pl.ds(row, TILE), :] = jnp.where(odd, low, high)
            return carry

        lax.fori_loop(0, nx * tiles, place, 0, unroll=4)
        x_copies = links(
            "gx", number,
            (
                (buf.at[:, pl.ds(first(nx), ny), :], buf.at[:, pl.ds(first(0), ny), :]),
                (buf.at[:, pl.ds(first(1), ny), :], buf.at[:, pl.ds(first(nx + 1), ny), :]),
            ),
        )
        start("gx", x_copies)
        yield
        below, above = has("gx")

        def blank(x):
            for field in range(fields + 1):
                buf[field, pl.ds(first(x), ny), :] = jnp.zeros((ny, LANES), buf.dtype)

        pl.when(jnp.logical_not(below))(functools.partial(blank, 0))
        pl.when(jnp.logical_not(above))(functools.partial(blank, nx + 1))
        finish("gx", x_copies)

        chunks = [(x, min(TILE, planes - x)) for x in range(0, planes, TILE)]

        def gather(field, carry):
            for x, count in chunks:
                ys[0, field, pl.ds(x, count), :] = buf[field, pl.ds(first(x) + ny - 1, count, stride=pitch), :]
                ys[1, field, pl.ds(x, count), :] = buf[field, pl.ds(first(x), count, stride=pitch), :]
            return carry

        lax.fori_loop(0, fields + 1, gather, 0)
        y_copies = links("gy", number, ((ys.at[0], yr.at[0]), (ys.at[1], yr.at[1])))
        start("gy", y_copies)
        yield
        finish("gy", y_copies)
        below, above = has("gy")

        def spread(field, carry):
            for x, count in chunks:
                blank_rows = jnp.zeros((count, LANES), buf.dtype)
                low = jnp.where(below, yr[0, field, pl.ds(x, count), :], blank_rows)
                high = jnp.where(above, yr[1, field, pl.ds(x, count), :], blank_rows)
                buf[field, pl.ds(first(x) - 1, count, stride=pitch), :] = low
                buf[field, pl.ds(first(x) + ny, count, stride=pitch), :] = high
            return carry

        lax.fori_loop(0, fields + 1, spread, 0)
        yield

    def shift(buf, to_left, to_right, fields):
        def body(g, carry):
            at = [pl.ds(pl.multiple_of((g * GROUP + k) * TILE, TILE), TILE) for k in range(GROUP)]
            ends = [buf[fields, near, :] for near in at]
            for field in range(fields):
                end = [e if field == 0 else pltpu.roll(e, LANES - 2 * field, 1) for e in ends]
                for near, e in zip(at, end):
                    value = buf[field, near, :]
                    to_left[field, near, :] = pltpu.roll(jnp.where(lane == LANES - 1, e, value), 1, 1)
                    to_right[field, near, :] = pltpu.roll(jnp.where(lane == 0, e, value), LANES - 1, 1)
            return carry

        lax.fori_loop(0, rows // (GROUP * TILE), body, 0)

    def fill(t, carry):
        row, at = own_tile(t)
        own = pl.ds(at, TILE)
        value = jnp.where(flag[own, :] == 1, code[own, :] | CENTER, CENTER)
        codes[0, pl.ds(row, TILE), :] = value
        zs_i[own, :] = pack(None, value, 0)
        return carry

    count = nx * tiles

    def loop(body, part=0, parts=1, unroll=2):
        low, high = (count * k // (4 * parts) * 4 for k in (part, part + 1))
        if part == parts - 1:
            high = count
        lax.fori_loop(low, high, body, 0, unroll=unroll)

    cut = nspec // 2
    group_a, group_b = list(range(cut)), list(range(cut, nspec))

    def fractions(own):
        is_cut = flag[own, :] == 1
        volume = jnp.where(is_cut, vol[own, :], 256).astype(jnp.float32) * (1.0 / 256.0)
        face = jnp.where(is_cut, area[own, :], 256).astype(jnp.float32) * (1.0 / 256.0)
        return volume, face

    def peer_copies(axis):
        n = size[axis]
        number = AXES.index(axis)
        return [
            pltpu.make_async_remote_copy(
                src_ref=peers.at[number, here[axis]], dst_ref=peers.at[number, here[axis]],
                send_sem=peer_send.at[number, k], recv_sem=peer_recv.at[number, k],
                device_id={axis: lax.rem(here[axis] + k, n)}, device_id_type=MESH,
            )
            for k in range(1, n)
        ]

    def reduce_start(axis, value):
        peers[AXES.index(axis), here[axis]] = value
        for copy in peer_copies(axis):
            copy.start()

    def reduce_finish(axis):
        number = AXES.index(axis)
        for copy in peer_copies(axis):
            copy.wait()
        value = peers[number, 0]
        for k in range(1, size[axis]):
            value = value + peers[number, k]
        return value

    loop(fill, unroll=4)
    code_steps = exchange(0, codes, zs_i, zl_i, zr_i, ys_i, yr_i, 1)
    next(code_steps)
    sums[...] = jnp.zeros(sums.shape, jnp.float32)

    def add_up(t, totals):
        _, at = own_tile(t)
        own = pl.ds(at, TILE)
        volume, _ = fractions(own)
        return tuple(totals[s] + volume * prov[s, own, :] for s in range(nspec))

    totals = lax.fori_loop(0, count, add_up, tuple(jnp.zeros((TILE, LANES), jnp.float32) for _ in range(nspec)))
    for s in range(nspec):
        sums[s] = totals[s]
    next(code_steps)
    local = jnp.concatenate(
        [jnp.sum(sums[s], axis=0, keepdims=True) for s in range(nspec)]
        + [jnp.zeros((peers.shape[2] - nspec, LANES), jnp.float32)],
        axis=0,
    )
    reduce_start("gx", local)
    next(code_steps)
    next(code_steps)
    shift(codes, codes_l, codes_r, 1)
    code_at = {-1: codes_l, 0: codes, 1: codes_r}

    def weigh_a(t, carry):
        row, at = own_tile(t)
        own = pl.ds(at, TILE)
        counted = jnp.zeros((TILE, LANES), jnp.int32)
        for position, (a, b, c) in enumerate(OFFSETS):
            near = code_at[-c][0, pl.ds(row - a * pitch - b, TILE), :]
            counted = counted + (lax.shift_right_logical(near, position) & 1)
        volume, face = fractions(own)
        share = 1.0 / counted.astype(jnp.float32)
        scaling[own, :] = face * share
        weight = volume * share
        weights[own, :] = weight
        packed = None
        for f, s in enumerate(group_a):
            value = weight * prov[s, own, :]
            carried_a[f, pl.ds(row, TILE), :] = value
            packed = pack(packed, value, f)
        value = weight * face
        carried_a[cut, pl.ds(row, TILE), :] = value
        zs_f[0, own, :] = pack(packed, value, cut)
        return carry

    def weigh_b(t, carry):
        row, at = own_tile(t)
        own = pl.ds(at, TILE)
        weight = weights[own, :]
        packed = None
        for f, s in enumerate(group_b):
            value = weight * prov[s, own, :]
            carried_b[f, pl.ds(row, TILE), :] = value
            packed = pack(packed, value, f)
        zs_f[1, own, :] = packed
        return carry

    def exchange_f(number, buf, fields):
        k = number - 1
        return exchange(
            number, buf, zs_f.at[k], zl_f.at[k], zr_f.at[k],
            ys_f.at[k, :, pl.ds(0, fields + 1)], yr_f.at[k, :, pl.ds(0, fields + 1)], fields,
        )

    def taps(t, fields, at_shift, sign):
        row, _ = own_tile(t)
        zero = jnp.zeros((TILE, LANES), jnp.float32)
        found = [zero] * fields
        mine = codes[0, pl.ds(row, TILE), :] if sign > 0 else None
        for position, (a, b, c) in enumerate(OFFSETS):
            near = pl.ds(row + sign * (a * pitch + b), TILE)
            code_here = mine if sign > 0 else code_at[-c][0, near, :]
            present = (code_here & (1 << position)) != 0
            for f in range(fields):
                found[f] = found[f] + jnp.where(present, at_shift[sign * c][f, near, :], zero)
        return found

    def quota_a(t, carry):
        row, at = own_tile(t)
        found = taps(t, cut + 1, {-1: left_a, 0: carried_a, 1: right_a}, 1)
        inverted = 1.0 / found[cut]
        inverse[pl.ds(at, TILE), :] = inverted
        packed = None
        for f in range(cut):
            value = found[f] * inverted
            quotas_a[f, pl.ds(row, TILE), :] = value
            packed = pack(packed, value, f)
        zs_f[2, pl.ds(at, TILE), :] = packed
        return carry

    def quota_b(t, carry):
        row, at = own_tile(t)
        found = taps(t, len(group_b), {-1: left_b, 0: carried_b, 1: right_b}, 1)
        inverted = inverse[pl.ds(at, TILE), :]
        packed = None
        for f in range(len(group_b)):
            value = found[f] * inverted
            quotas_b[f, pl.ds(row, TILE), :] = value
            packed = pack(packed, value, f)
        zs_f[3, pl.ds(at, TILE), :] = packed
        return carry

    def scatter(group, buf, left, right, t, carry):
        _, at = own_tile(t)
        own = pl.ds(at, TILE)
        found = taps(t, len(group), {-1: left, 0: buf, 1: right}, -1)
        factor = scaling[own, :]
        for f, s in enumerate(group):
            out[s, own, :] = factor * found[f]
        return carry

    scatter_a = functools.partial(scatter, group_a, quotas_a, left_a, right_a)
    scatter_b = functools.partial(scatter, group_b, quotas_b, left_b, right_b)

    loop(weigh_a)
    steps_a = exchange_f(1, carried_a, cut + 1)
    next(steps_a)
    loop(weigh_b)
    steps_b = exchange_f(2, carried_b, len(group_b))
    next(steps_b)
    next(steps_a)
    next(steps_b)
    reduce_start("gy", reduce_finish("gx"))
    next(steps_a)
    next(steps_b)
    next(steps_a)
    shift(carried_a, left_a, right_a, cut + 1)
    loop(quota_a)
    steps_qa = exchange_f(3, quotas_a, cut)
    next(steps_qa)
    next(steps_b)
    shift(carried_b, left_b, right_b, len(group_b))
    next(steps_qa)
    loop(quota_b, 0, 2)
    next(steps_qa)
    loop(quota_b, 1, 2)
    steps_qb = exchange_f(4, quotas_b, len(group_b))
    next(steps_qb)
    reduce_start("gz", reduce_finish("gy"))
    next(steps_qa)
    next(steps_qb)
    shift(quotas_a, left_a, right_a, cut)
    next(steps_qb)
    loop(scatter_a)
    summed = reduce_finish("gz")
    change[...] = jnp.broadcast_to(jnp.sum(summed, axis=1, keepdims=True) * scale, change.shape)
    next(steps_qb)
    shift(quotas_b, left_b, right_b, len(group_b))
    loop(scatter_b)


def per_device(provisional, cut_flag, cut_code, volume_level, area_level):
    nspec, nx, ny, nz = provisional.shape
    assert nz == LANES and ny % TILE == 0
    own = nx * ny
    planes = nx + 2
    rows = -(-(TILE + planes * (ny + TILE)) // (GROUP * TILE)) * (GROUP * TILE)
    slab = -(-planes // TILE) * TILE
    most = max(lax.axis_size(axis) for axis in AXES)
    cells = own * nz * math.prod(lax.axis_size(axis) for axis in AXES)
    high = -(-nspec // TILE) * TILE
    cut = nspec // 2
    rest = nspec - cut
    f32, i32 = jnp.float32, jnp.int32
    vmem = pl.BlockSpec(memory_space=pltpu.VMEM)
    shapes = [
        ((2, rows, nz), i32), ((1, rows, nz), i32), ((1, rows, nz), i32),
        ((cut + 2, rows, nz), f32), ((rest + 1, rows, nz), f32),
        ((cut + 1, rows, nz), f32), ((rest + 1, rows, nz), f32),
        ((cut + 1, rows, nz), f32), ((cut + 1, rows, nz), f32),
        ((rest, rows, nz), f32), ((rest, rows, nz), f32),
        ((own, nz), f32), ((own, nz), f32), ((own, nz), f32),
        ((own, nz), i32), ((own, nz), i32), ((own, nz), i32),
        ((4, own, nz), f32), ((4, own, nz), f32), ((4, own, nz), f32),
        ((2, 2, slab, nz), i32), ((2, 2, slab, nz), i32),
        ((4, 2, rest + 1, slab, nz), f32), ((4, 2, rest + 1, slab, nz), f32),
        ((nspec, TILE, nz), f32), ((3, most, high, nz), f32),
    ]
    out, change = pl.pallas_call(
        functools.partial(kernel, nx, ny, 1.0 / math.sqrt(cells)),
        out_shape=(
            jax.ShapeDtypeStruct((nspec, own, nz), f32),
            jax.ShapeDtypeStruct((high, nz), f32),
        ),
        in_specs=[vmem] * 5,
        out_specs=(vmem, vmem),
        scratch_shapes=[pltpu.VMEM(shape, kind) for shape, kind in shapes]
        + [
            pltpu.SemaphoreType.DMA((5, 6)), pltpu.SemaphoreType.DMA((5, 6)),
            pltpu.SemaphoreType.DMA((3, most)), pltpu.SemaphoreType.DMA((3, most)),
        ],
        compiler_params=pltpu.CompilerParams(
            collective_id=0, has_side_effects=True, vmem_limit_bytes=60 * 1024 * 1024
        ),
    )(
        provisional.reshape(nspec, own, nz),
        cut_flag.reshape(own, nz),
        cut_code.reshape(own, nz),
        volume_level.reshape(own, nz),
        area_level.reshape(own, nz),
    )
    return out.reshape(provisional.shape), change[:nspec, 0]


def solution(mesh):
    spec = P("gx", "gy", "gz")
    wide = P(None, "gx", "gy", "gz")
    return jax.shard_map(
        per_device, mesh=mesh, in_specs=(wide, spec, spec, spec, spec), out_specs=(wide, P()), check_vma=False
    )
```

```python
import functools
import math

import jax
import jax.numpy as jnp
from jax import lax
from jax.experimental import pallas as pl
from jax.experimental.pallas import tpu as pltpu
from jax.sharding import PartitionSpec as P

CENTER = 8192
OFFSETS = [(a, b, c) for a in (-1, 0, 1) for b in (-1, 0, 1) for c in (-1, 0, 1)]
AXES = ("gx", "gy", "gz")
MESH = pl.DeviceIdType.MESH
LANES = 128
TILE = 8
GROUP = 16


def kernel(
    nx, ny, scale,
    prov, flag, code, vol, area,
    out, change,
    codes, codes_l, codes_r, carried_a, carried_b, quotas_a, quotas_b, left_a, right_a, left_b, right_b,
    scaling, weights, inverse,
    zs_i, zl_i, zr_i, zs_f, zl_f, zr_f, ys_i, yr_i, ys_f, yr_f, peers,
    send, recv, peer_send, peer_recv,
):
    nspec = prov.shape[0]
    pitch = ny + TILE
    planes = nx + 2
    rows = codes.shape[1]
    tiles = ny // TILE
    here = {axis: lax.axis_index(axis) for axis in AXES}
    size = {axis: lax.axis_size(axis) for axis in AXES}
    lane = lax.broadcasted_iota(jnp.int32, (TILE, LANES), 1)

    barrier = pltpu.get_barrier_semaphore()
    for axis in AXES:
        for k in range(1, size[axis]):
            pl.semaphore_signal(
                barrier, inc=1, device_id={axis: lax.rem(here[axis] + k, size[axis])}, device_id_type=MESH
            )
    pl.semaphore_wait(barrier, sum(size[axis] - 1 for axis in AXES))

    def first(x):
        return TILE + x * pitch

    def own_tile(t):
        row = TILE + (t // tiles + 1) * pitch + lax.rem(t, tiles) * TILE
        return pl.multiple_of(row, TILE), pl.multiple_of(t * TILE, TILE)

    def links(axis, exchange, pairs):
        number = 2 * AXES.index(axis)
        n = size[axis]
        copies = []
        for way, (source, landing) in enumerate(pairs):
            step = 1 if way == 0 else n - 1
            copies.append(
                pltpu.make_async_remote_copy(
                    src_ref=source, dst_ref=landing,
                    send_sem=send.at[exchange, number + way], recv_sem=recv.at[exchange, number + way],
                    device_id={axis: lax.rem(here[axis] + step, n)}, device_id_type=MESH,
                )
            )
        return copies

    def has(axis):
        return here[axis] > 0, here[axis] < size[axis] - 1

    def start(axis, copies):
        below, above = has(axis)
        pl.when(above)(copies[0].start)
        pl.when(below)(copies[1].start)

    def finish(axis, copies):
        below, above = has(axis)
        pl.when(above)(copies[0].wait_send)
        pl.when(below)(copies[0].wait_recv)
        pl.when(below)(copies[1].wait_send)
        pl.when(above)(copies[1].wait_recv)

    def pack(packed, value, field):
        if packed is None:
            packed = jnp.zeros_like(value)
        keep = (lane == 2 * field) | (lane == (2 * field + LANES - 1) % LANES)
        rolled = value if field == 0 else pltpu.roll(value, 2 * field, 1)
        return jnp.where(keep, rolled, packed)

    def exchange(number, buf, zs, zl, zr, ys, yr, fields):
        zero = jnp.zeros((TILE, LANES), buf.dtype)
        z_copies = links("gz", number, ((zs, zl), (zs, zr)))
        start("gz", z_copies)
        yield
        finish("gz", z_copies)
        below, above = has("gz")
        odd = (lane & 1) == 1

        def place(t, carry):
            row, at = own_tile(t)
            low = jnp.where(below, zl[pl.ds(at, TILE), :], zero)
            high = jnp.where(above, zr[pl.ds(at, TILE), :], zero)
            buf[fields, pl.ds(row, TILE), :] = jnp.where(odd, low, high)
            return carry

        lax.fori_loop(0, nx * tiles, place, 0, unroll=4)
        x_copies = links(
            "gx", number,
            (
                (buf.at[:, pl.ds(first(nx), ny), :], buf.at[:, pl.ds(first(0), ny), :]),
                (buf.at[:, pl.ds(first(1), ny), :], buf.at[:, pl.ds(first(nx + 1), ny), :]),
            ),
        )
        start("gx", x_copies)
        yield
        below, above = has("gx")

        def blank(x):
            for field in range(fields + 1):
                buf[field, pl.ds(first(x), ny), :] = jnp.zeros((ny, LANES), buf.dtype)

        pl.when(jnp.logical_not(below))(functools.partial(blank, 0))
        pl.when(jnp.logical_not(above))(functools.partial(blank, nx + 1))
        finish("gx", x_copies)

        chunks = [(x, min(TILE, planes - x)) for x in range(0, planes, TILE)]

        def gather(field, carry):
            for x, count in chunks:
                ys[0, field, pl.ds(x, count), :] = buf[field, pl.ds(first(x) + ny - 1, count, stride=pitch), :]
                ys[1, field, pl.ds(x, count), :] = buf[field, pl.ds(first(x), count, stride=pitch), :]
            return carry

        lax.fori_loop(0, fields + 1, gather, 0)
        y_copies = links("gy", number, ((ys.at[0], yr.at[0]), (ys.at[1], yr.at[1])))
        start("gy", y_copies)
        yield
        finish("gy", y_copies)
        below, above = has("gy")

        def spread(field, carry):
            for x, count in chunks:
                blank_rows = jnp.zeros((count, LANES), buf.dtype)
                low = jnp.where(below, yr[0, field, pl.ds(x, count), :], blank_rows)
                high = jnp.where(above, yr[1, field, pl.ds(x, count), :], blank_rows)
                buf[field, pl.ds(first(x) - 1, count, stride=pitch), :] = low
                buf[field, pl.ds(first(x) + ny, count, stride=pitch), :] = high
            return carry

        lax.fori_loop(0, fields + 1, spread, 0)
        yield

    def shift(buf, to_left, to_right, fields):
        def body(g, carry):
            at = [pl.ds(pl.multiple_of((g * GROUP + k) * TILE, TILE), TILE) for k in range(GROUP)]
            ends = [buf[fields, near, :] for near in at]
            for field in range(fields):
                end = [(pltpu.roll(e, (LANES + 1 - 2 * field) % LANES, 1), pltpu.roll(e, (2 * LANES - 1 - 2 * field) % LANES, 1)) for e in ends]
                for near, e in zip(at, end):
                    value = buf[field, near, :]
                    to_left[field, near, :] = jnp.where(lane == 0, e[0], pltpu.roll(value, 1, 1))
                    to_right[field, near, :] = jnp.where(lane == LANES - 1, e[1], pltpu.roll(value, LANES - 1, 1))
            return carry

        lax.fori_loop(0, rows // (GROUP * TILE), body, 0)

    def fill(t, carry):
        row, at = own_tile(t)
        own = pl.ds(at, TILE)
        value = jnp.where(flag[own, :] == 1, code[own, :] | CENTER, CENTER)
        codes[0, pl.ds(row, TILE), :] = value
        zs_i[own, :] = pack(None, value, 0)
        return carry

    count = nx * tiles

    def loop(body, part=0, parts=1, unroll=4):
        low, high = (count * k // (4 * parts) * 4 for k in (part, part + 1))
        if part == parts - 1:
            high = count
        lax.fori_loop(low, high, body, 0, unroll=unroll)

    cut = nspec // 2
    group_a, group_b = list(range(cut)), list(range(cut, nspec))

    def fractions(own):
        is_cut = flag[own, :] == 1
        volume = jnp.where(is_cut, vol[own, :], 256).astype(jnp.float32) * (1.0 / 256.0)
        face = jnp.where(is_cut, area[own, :], 256).astype(jnp.float32) * (1.0 / 256.0)
        return volume, face

    def peer_copies(axis):
        n = size[axis]
        number = AXES.index(axis)
        return [
            pltpu.make_async_remote_copy(
                src_ref=peers.at[number, here[axis]], dst_ref=peers.at[number, here[axis]],
                send_sem=peer_send.at[number, k], recv_sem=peer_recv.at[number, k],
                device_id={axis: lax.rem(here[axis] + k, n)}, device_id_type=MESH,
            )
            for k in range(1, n)
        ]

    def reduce_start(axis, value):
        peers[AXES.index(axis), here[axis]] = value
        for copy in peer_copies(axis):
            copy.start()

    def reduce_finish(axis):
        number = AXES.index(axis)
        for copy in peer_copies(axis):
            copy.wait()
        value = peers[number, 0]
        for k in range(1, size[axis]):
            value = value + peers[number, k]
        return value

    loop(fill, unroll=4)
    code_steps = exchange(0, codes, zs_i, zl_i, zr_i, ys_i, yr_i, 1)
    next(code_steps)

    def add_up(t, totals):
        _, at = own_tile(t)
        own = pl.ds(at, TILE)
        volume, _ = fractions(own)
        return tuple(totals[s] + volume * prov[s, own, :] for s in range(nspec))

    def add_part(part, totals):
        low, high = (count * k // 12 * 4 for k in (part, part + 1))
        return lax.fori_loop(low, high if part < 2 else count, add_up, totals, unroll=4)

    totals = tuple(jnp.zeros((TILE, LANES), jnp.float32) for _ in range(nspec))
    for part in range(3):
        totals = add_part(part, totals)
        next(code_steps)
    local = jnp.concatenate(
        [jnp.sum(total, axis=0, keepdims=True) for total in totals]
        + [jnp.zeros((peers.shape[2] - nspec, LANES), jnp.float32)],
        axis=0,
    )
    reduce_start("gx", local)
    shift(codes, codes_l, codes_r, 1)
    code_at = {-1: codes_l, 0: codes, 1: codes_r}

    def weigh_a(t, carry):
        row, at = own_tile(t)
        own = pl.ds(at, TILE)
        counted = jnp.zeros((TILE, LANES), jnp.int32)
        for position, (a, b, c) in enumerate(OFFSETS):
            near = code_at[-c][0, pl.ds(row - a * pitch - b, TILE), :]
            counted = counted + (lax.shift_right_logical(near, position) & 1)
        volume, face = fractions(own)
        share = 1.0 / counted.astype(jnp.float32)
        scaling[own, :] = face * share
        weight = volume * share
        weights[own, :] = weight
        packed = None
        for f, s in enumerate(group_a):
            value = weight * prov[s, own, :]
            carried_a[f, pl.ds(row, TILE), :] = value
            packed = pack(packed, value, f)
        value = weight * face
        carried_a[cut, pl.ds(row, TILE), :] = value
        zs_f[0, own, :] = pack(packed, value, cut)
        return carry

    def weigh_b(t, carry):
        row, at = own_tile(t)
        own = pl.ds(at, TILE)
        weight = weights[own, :]
        packed = None
        for f, s in enumerate(group_b):
            value = weight * prov[s, own, :]
            carried_b[f, pl.ds(row, TILE), :] = value
            packed = pack(packed, value, f)
        zs_f[1, own, :] = packed
        return carry

    def exchange_f(number, buf, fields):
        k = number - 1
        return exchange(
            number, buf, zs_f.at[k], zl_f.at[k], zr_f.at[k],
            ys_f.at[k, :, pl.ds(0, fields + 1)], yr_f.at[k, :, pl.ds(0, fields + 1)], fields,
        )

    def taps(t, fields, at_shift, sign):
        row, _ = own_tile(t)
        zero = jnp.zeros((TILE, LANES), jnp.float32)
        found = [zero] * fields
        mine = codes[0, pl.ds(row, TILE), :] if sign > 0 else None
        for position, (a, b, c) in enumerate(OFFSETS):
            near = pl.ds(row + sign * (a * pitch + b), TILE)
            code_here = mine if sign > 0 else code_at[-c][0, near, :]
            present = (code_here & (1 << position)) != 0
            for f in range(fields):
                found[f] = found[f] + jnp.where(present, at_shift[sign * c][f, near, :], zero)
        return found

    def quota_a(t, carry):
        row, at = own_tile(t)
        found = taps(t, cut + 1, {-1: left_a, 0: carried_a, 1: right_a}, 1)
        inverted = 1.0 / found[cut]
        inverse[pl.ds(at, TILE), :] = inverted
        packed = None
        for f in range(cut):
            value = found[f] * inverted
            quotas_a[f, pl.ds(row, TILE), :] = value
            packed = pack(packed, value, f)
        zs_f[2, pl.ds(at, TILE), :] = packed
        return carry

    def quota_b(t, carry):
        row, at = own_tile(t)
        found = taps(t, len(group_b), {-1: left_b, 0: carried_b, 1: right_b}, 1)
        inverted = inverse[pl.ds(at, TILE), :]
        packed = None
        for f in range(len(group_b)):
            value = found[f] * inverted
            quotas_b[f, pl.ds(row, TILE), :] = value
            packed = pack(packed, value, f)
        zs_f[3, pl.ds(at, TILE), :] = packed
        return carry

    def scatter(group, buf, left, right, t, carry):
        _, at = own_tile(t)
        own = pl.ds(at, TILE)
        found = taps(t, len(group), {-1: left, 0: buf, 1: right}, -1)
        factor = scaling[own, :]
        for f, s in enumerate(group):
            out[s, own, :] = factor * found[f]
        return carry

    scatter_a = functools.partial(scatter, group_a, quotas_a, left_a, right_a)
    scatter_b = functools.partial(scatter, group_b, quotas_b, left_b, right_b)

    loop(weigh_a)
    steps_a = exchange_f(1, carried_a, cut + 1)
    next(steps_a)
    loop(weigh_b)
    steps_b = exchange_f(2, carried_b, len(group_b))
    next(steps_b)
    next(steps_a)
    next(steps_b)
    reduce_start("gy", reduce_finish("gx"))
    next(steps_a)
    next(steps_b)
    next(steps_a)
    shift(carried_a, left_a, right_a, cut + 1)
    loop(quota_a)
    steps_qa = exchange_f(3, quotas_a, cut)
    next(steps_qa)
    next(steps_b)
    shift(carried_b, left_b, right_b, len(group_b))
    next(steps_qa)
    loop(quota_b, 0, 2)
    next(steps_qa)
    loop(quota_b, 1, 2)
    steps_qb = exchange_f(4, quotas_b, len(group_b))
    next(steps_qb)
    reduce_start("gz", reduce_finish("gy"))
    next(steps_qa)
    next(steps_qb)
    shift(quotas_a, left_a, right_a, cut)
    next(steps_qb)
    loop(scatter_a)
    summed = reduce_finish("gz")
    change[...] = jnp.broadcast_to(jnp.sum(summed, axis=1, keepdims=True) * scale, change.shape)
    next(steps_qb)
    shift(quotas_b, left_b, right_b, len(group_b))
    loop(scatter_b)


def per_device(provisional, cut_flag, cut_code, volume_level, area_level):
    nspec, nx, ny, nz = provisional.shape
    assert nz == LANES and ny % TILE == 0
    own = nx * ny
    planes = nx + 2
    rows = -(-(TILE + planes * (ny + TILE)) // (GROUP * TILE)) * (GROUP * TILE)
    slab = -(-planes // TILE) * TILE
    most = max(lax.axis_size(axis) for axis in AXES)
    cells = own * nz * math.prod(lax.axis_size(axis) for axis in AXES)
    high = -(-nspec // TILE) * TILE
    cut = nspec // 2
    rest = nspec - cut
    f32, i32 = jnp.float32, jnp.int32
    vmem = pl.BlockSpec(memory_space=pltpu.VMEM)
    shapes = [
        ((2, rows, nz), i32), ((1, rows, nz), i32), ((1, rows, nz), i32),
        ((cut + 2, rows, nz), f32), ((rest + 1, rows, nz), f32),
        ((cut + 1, rows, nz), f32), ((rest + 1, rows, nz), f32),
        ((cut + 1, rows, nz), f32), ((cut + 1, rows, nz), f32),
        ((rest, rows, nz), f32), ((rest, rows, nz), f32),
        ((own, nz), f32), ((own, nz), f32), ((own, nz), f32),
        ((own, nz), i32), ((own, nz), i32), ((own, nz), i32),
        ((4, own, nz), f32), ((4, own, nz), f32), ((4, own, nz), f32),
        ((2, 2, slab, nz), i32), ((2, 2, slab, nz), i32),
        ((4, 2, rest + 1, slab, nz), f32), ((4, 2, rest + 1, slab, nz), f32),
        ((3, most, high, nz), f32),
    ]
    out, change = pl.pallas_call(
        functools.partial(kernel, nx, ny, 1.0 / math.sqrt(cells)),
        out_shape=(
            jax.ShapeDtypeStruct((nspec, own, nz), f32),
            jax.ShapeDtypeStruct((high, nz), f32),
        ),
        in_specs=[vmem] * 5,
        out_specs=(vmem, vmem),
        scratch_shapes=[pltpu.VMEM(shape, kind) for shape, kind in shapes]
        + [
            pltpu.SemaphoreType.DMA((5, 6)), pltpu.SemaphoreType.DMA((5, 6)),
            pltpu.SemaphoreType.DMA((3, most)), pltpu.SemaphoreType.DMA((3, most)),
        ],
        compiler_params=pltpu.CompilerParams(
            collective_id=0, has_side_effects=True, vmem_limit_bytes=60 * 1024 * 1024
        ),
    )(
        provisional.reshape(nspec, own, nz),
        cut_flag.reshape(own, nz),
        cut_code.reshape(own, nz),
        volume_level.reshape(own, nz),
        area_level.reshape(own, nz),
    )
    return out.reshape(provisional.shape), change[:nspec, 0]


def solution(mesh):
    spec = P("gx", "gy", "gz")
    wide = P(None, "gx", "gy", "gz")
    return jax.shard_map(
        per_device, mesh=mesh, in_specs=(wide, spec, spec, spec, spec), out_specs=(wide, P()), check_vma=False
    )
```
